256 devices in a mesh: pipe: 4 (over z_lo, core), seq: 16 (over x, z_hi), head: 4 (over y).
Axes of the slice: x: 4, y: 4, z: 8 (z_hi: 4, z_lo: 2; z = z_hi * 2 + z_lo), core: 2. Of those that a mesh axis runs over, the one named last changes fastest.
Arguments:
- section_input: bfloat16 [4, 2048, 3, 2048], P('pipe', ('seq', 'head')), may hold values from -8 to 8
- grad_input: bfloat16 [4, 2048, 2048], P('pipe', ('seq', 'head')), may hold values from -6 to 6
- strided_blocks: int32 [16, 14], replicated, may hold values from 0 to 13, as said below
- strided_count: int32 [16], replicated, may hold values from 0 to 14, as said below
Outputs:
- attn_out: bfloat16 [4, 2048, 2048], P('pipe', ('seq', 'head'))
- grad_qkv: bfloat16 [4, 2048, 3, 2048], P('pipe', ('seq', 'head'))
The draws below stay inside these ranges and needn't reach their ends.
Inputs may be any that keep to these rules, and one draw needn't show every extreme that they name: `strided_blocks`: row b holds in its first strided_count[b] entries distinct key blocks, each below b - 1; its other entries are 0 and unused. strided_count[b] is at most min(14, b - 1) for b >= 1 and 0 for b = 0; the last query block lists exactly 14.
All inputs are finite; a program needn't handle non-finite values.
Results may differ from the reference program's by a relative error of at most 0.0081.
Values may be sent and summed in bfloat16 or wider, within the bound.
A program may use at most 128 MiB of HBM per device.

```python
import math
import jax
import jax.numpy as jnp
from jax import lax

HEADS = 16
HD = 128
BLK = 128
SEQ = 2048
NB = 16
SMAX = 14
N_PIPE = 4


def strided_tables(key):
    count_key = jax.random.fold_in(key, 7)
    score_key = jax.random.fold_in(key, 11)
    block_ids = jnp.arange(NB, dtype=jnp.int32)
    ceiling = jnp.clip(block_ids - 1, 0, SMAX)
    lowest = (ceiling + 1) // 2
    counts = jax.random.randint(count_key, (NB,), lowest, ceiling + 1)
    counts = jnp.where(block_ids == NB - 1, SMAX, counts).astype(jnp.int32)
    columns = jnp.arange(NB, dtype=jnp.int32)
    raw_scores = jax.random.randint(score_key, (NB, NB), 0, 2 ** 20) * NB + columns[None, :]
    allowed = columns[None, :] < block_ids[:, None] - 1
    raw_scores = jnp.where(allowed, raw_scores, raw_scores + 2 ** 30)
    forced = (block_ids[:, None] == NB - 1) & (columns[None, :] == NB - 3)
    raw_scores = jnp.where(forced, -1, raw_scores)
    picked_cols = jnp.argsort(raw_scores, axis=1)[:, :SMAX]
    slot_used = jnp.arange(SMAX)[None, :] < counts[:, None]
    listed = jnp.where(slot_used, picked_cols, 0).astype(jnp.int32)
    return (listed, counts)


def draw_strided_blocks(key, part):
    return strided_tables(key)[0]


def draw_strided_count(key, part):
    return strided_tables(key)[1]


def draw_section_input(key, part):
    feat_width = HEADS * HD
    base_key = jax.random.fold_in(key, 0)
    component = jnp.array([1.5, 1.5, 1.0], jnp.float32)[None, None, :, None]
    values = jax.random.normal(base_key, (N_PIPE, SEQ, 3, feat_width), jnp.float32) * component
    return jnp.clip(values, -8.0, 8.0).astype(jnp.bfloat16)


def shard_levels(own_key, shape, shards, low, top_value):
    factor_of, own = 1.0, jax.random.fold_in(own_key, 6)
    for dim, shards_of in shards:
        draws = jnp.exp(jax.random.uniform(jax.random.fold_in(own, dim), (shards_of,), jnp.float32, low / len(shards), top_value / len(shards)))
        factor_of = factor_of * jnp.repeat(draws, shape[dim] // shards_of).reshape([-1 if axis == dim else 1 for axis in range(len(shape))])
    return factor_of


def bell_draw(stream_key, extent, width, most, shards=(), kind=jnp.bfloat16):
    values = width * jax.random.normal(stream_key, extent, jnp.float32)
    if shards:
        values = values * shard_levels(stream_key, extent, shards, -0.22, 0.18)
    return jnp.clip(values, -most, most).astype(kind)


def setup_inputs(seed: int = 0) -> dict:
    keys = jax.random.split(jax.random.key(seed), 5)
    section_input = draw_section_input(jax.random.fold_in(keys[4], 71), 0)
    grad_input = bell_draw(keys[1], (N_PIPE, SEQ, HEADS * HD), 1.0, 6.0, ((0, 4), (1, 64)))
    strided_blocks = draw_strided_blocks(jax.random.fold_in(keys[4], 71), 0)
    strided_count = draw_strided_count(jax.random.fold_in(keys[4], 71), 0)
    return {"section_input": section_input, "grad_input": grad_input, "strided_blocks": strided_blocks, "strided_count": strided_count}


def slot_table(block_id, strided_blocks, strided_count):
    listed = strided_blocks[block_id].astype(jnp.int32)
    first_slot = jnp.reshape(block_id, (1,)).astype(jnp.int32)
    second_slot = jnp.reshape(jnp.maximum(block_id - 1, 0), (1,)).astype(jnp.int32)
    slot_index = jnp.concatenate([first_slot, second_slot, listed])
    slot_valid = jnp.concatenate([jnp.ones((1,), bool), jnp.reshape(block_id >= 1, (1,)), jnp.arange(SMAX) < strided_count[block_id]])
    return (slot_index, slot_valid)

def section_pass(qkv_rows, grad_rows, strided_blocks, strided_count):
    feat_width = HEADS * HD
    att_scale = 1.0 / math.sqrt(HD)
    queries = qkv_rows[:, 0].reshape(NB, BLK, HEADS, HD).astype(jnp.float32)
    keys_all = qkv_rows[:, 1].reshape(NB, BLK, HEADS, HD).astype(jnp.float32)
    values_all = qkv_rows[:, 2].reshape(NB, BLK, HEADS, HD).astype(jnp.float32)
    grad_all = grad_rows.reshape(NB, BLK, HEADS, HD).astype(jnp.float32)
    causal = jnp.arange(BLK)[None, :] <= jnp.arange(BLK)[:, None]
    slot_first = jnp.arange(SMAX + 2) == 0

    def one_block(totals, block_id):
        slot_index, slot_valid = slot_table(block_id, strided_blocks, strided_count)
        keys_blk = keys_all[slot_index]
        values_blk = values_all[slot_index]
        query_blk = queries[block_id]
        grad_blk = grad_all[block_id]
        scores = jnp.einsum('qhd,nkhd->hqnk', query_blk, keys_blk) * att_scale
        keep_mask = slot_valid[None, None, :, None] & (~slot_first[None, None, :, None] | causal[None, :, None, :])
        row_max = lax.optimization_barrier(jnp.max(jnp.where(keep_mask, scores, -jnp.inf), axis=(2, 3)))
        row_total = lax.optimization_barrier(jnp.sum(jnp.where(keep_mask, jnp.exp(scores - row_max[:, :, None, None]), 0.0), axis=(2, 3)))
        log_total = row_max + jnp.log(row_total)
        weights = jnp.where(keep_mask, jnp.exp(scores - log_total[:, :, None, None]), 0.0)
        weights_half = lax.optimization_barrier(weights.astype(jnp.bfloat16)).astype(jnp.float32)
        attended = jnp.einsum('hqnk,nkhd->qhd', weights_half, values_blk)
        row_delta = lax.optimization_barrier(jnp.sum(grad_blk * attended, axis=-1)).T
        grad_w = jnp.einsum('qhd,nkhd->hqnk', grad_blk, values_blk)
        grad_s = weights * (grad_w - row_delta[:, :, None, None])
        grad_half = lax.optimization_barrier(grad_s.astype(jnp.bfloat16)).astype(jnp.float32)
        grad_query = jnp.einsum('hqnk,nkhd->qhd', grad_half, keys_blk) * att_scale
        grad_keys = jnp.einsum('hqnk,qhd->nkhd', grad_half, query_blk) * att_scale
        grad_values = jnp.einsum('hqnk,qhd->nkhd', weights_half, grad_blk)
        totals = totals.at[slot_index].add(jnp.stack([grad_keys, grad_values], axis=2))
        return (totals, (attended.astype(jnp.bfloat16), grad_query.astype(jnp.bfloat16)))
    start_totals = jnp.zeros((NB, BLK, 2, HEADS, HD), jnp.float32)
    totals, (outputs, grad_queries) = lax.scan(one_block, start_totals, jnp.arange(NB, dtype=jnp.int32))
    attn_rows = outputs.reshape(SEQ, feat_width)
    grad_keys = totals[:, :, 0].reshape(SEQ, feat_width).astype(jnp.bfloat16)
    grad_values = totals[:, :, 1].reshape(SEQ, feat_width).astype(jnp.bfloat16)
    grads = jnp.stack([grad_queries.reshape(SEQ, feat_width), grad_keys, grad_values], axis=1)
    return (attn_rows, grads)

def reference(section_input, grad_input, strided_blocks, strided_count):
    outputs = []
    gradients = []
    for section in range(N_PIPE):
        qkv_rows = section_input[(section - 1) % N_PIPE]
        grad_rows = grad_input[(section + 1) % N_PIPE]
        attn_rows, grads = section_pass(qkv_rows, grad_rows, strided_blocks, strided_count)
        outputs.append(attn_rows)
        gradients.append(grads)
    return (jnp.stack(outputs, axis=0), jnp.stack(gradients, axis=0))
```

```python
import math

import jax
import jax.numpy as jnp
from jax import lax
from jax.experimental import pallas as pl
from jax.experimental.pallas import tpu as pltpu
from jax.sharding import PartitionSpec as P

HD = 128
BLK = 128
TILE = 256
SEQ = 2048
NB = SEQ // BLK
NT = SEQ // TILE
N_PIPE = 4
N_SEQ = 16
N_HEAD = 4
HEADS = 16
ROWS = 32
SMAX = 14
SCALE = 1.0 / math.sqrt(HD)
SCALE2 = math.log2(math.e) / math.sqrt(HD)
NEG = -1e30
F32 = jnp.float32
BF16 = jnp.bfloat16
MESH = pl.DeviceIdType.MESH


def dot_nt(a, b):
    return lax.dot_general(a, b, (((1,), (1,)), ((), ())), preferred_element_type=F32)


def dot_nn(a, b):
    return lax.dot_general(a, b, (((1,), (0,)), ((), ())), preferred_element_type=F32)


def owner_of(section, head):
    x, y = head // 4, head % 4
    z_lo = 1 - section // 2
    z_hi = (x + (section % 2) * 2 + section // 2) % 4
    return (2 * z_lo + section % 2, x * 4 + z_hi, y)


def owned_by(pipe, seq, y):
    x, z_hi = seq // 4, seq % 4
    half = 1 - pipe // 2
    section = 2 * half + pipe % 2
    is_owner = z_hi == (x + (pipe % 2) * 2 + half) % 4
    return is_owner, section, x * 4 + y


def kept_words(blocks_ref, count_ref, words_ref):
    def one(b, _):
        word = jnp.where(b > 0, jnp.left_shift(1, jnp.maximum(b - 1, 0)), 0)
        for t in range(SMAX):
            bit = jnp.left_shift(1, blocks_ref[b, t])
            word = word | jnp.where(t < count_ref[b], bit, 0)
        words_ref[b] = word
        return 0

    lax.fori_loop(0, NB, one, 0)


def transposed(x_ref, kt_ref, vt_ref):
    def one(j, _):
        rows = pl.ds(pl.multiple_of(j * TILE, TILE), TILE)
        kt_ref[j] = x_ref[1, rows, :].T
        vt_ref[j] = x_ref[2, rows, :].T
        return 0

    lax.fori_loop(0, NT, one, 0)


def query_tile(b, bias, before_grad, x_ref, g_ref, kt_ref, vt_ref, s_ref, e_ref, dk_ref, dv_ref, o_ref, d_ref):
    rows_q = slice(b * TILE, (b + 1) * TILE)
    q = x_ref[0, rows_q, :]
    lane = lax.broadcasted_iota(jnp.int32, (1, TILE), 1)
    top = jnp.full((8, TILE), NEG, F32)
    for j in range(b + 1):
        s = dot_nt(x_ref[1, j * TILE : (j + 1) * TILE, :], q) * SCALE2
        if j == b:
            key = lax.broadcasted_iota(jnp.int32, (TILE, TILE), 0)
            query = lax.broadcasted_iota(jnp.int32, (TILE, TILE), 1)
            s = jnp.where(key <= query, s, NEG)
        else:
            halves = []
            for half in range(2):
                row = jnp.where(lane < BLK, bias(2 * b, 2 * j + half), bias(2 * b + 1, 2 * j + half))
                halves.append(s[half * BLK : (half + 1) * BLK] + row)
            s = jnp.concatenate(halves, axis=0)
        s_ref[j] = s
        top = jnp.maximum(top, jnp.max(s.reshape(TILE // 8, 8, TILE), axis=0))
    top = jnp.max(top, axis=0, keepdims=True)
    total = jnp.zeros((8, TILE), F32)
    out = jnp.zeros((HD, TILE), F32)
    for j in range(b + 1):
        e = jnp.exp2(s_ref[j] - top)
        total = total + jnp.sum(e.reshape(TILE // 8, 8, TILE), axis=0)
        e = e.astype(BF16)
        e_ref[j] = e
        out = out + dot_nn(vt_ref[j], e)
    inverse = 1.0 / jnp.sum(total, axis=0, keepdims=True)
    out = out * inverse
    before_grad()
    g = g_ref[rows_q, :]
    delta = jnp.sum(out * g.astype(F32).T, axis=0, keepdims=True)
    o_ref[rows_q, :] = out.T.astype(BF16)
    dq = jnp.zeros((HD, TILE), F32)
    for j in range(b + 1):
        rows_k = slice(j * TILE, (j + 1) * TILE)
        p = e_ref[j].astype(F32) * inverse
        dp = dot_nt(x_ref[2, rows_k, :], g)
        ds = (p * (dp - delta)).astype(BF16)
        dv = dot_nn(p.astype(BF16), g)
        dk = dot_nn(ds, q)
        if b == NT - 1:
            dv_ref[rows_k, :] = dv
            dk_ref[rows_k, :] = dk
        else:
            dv_ref[rows_k, :] += dv
            dk_ref[rows_k, :] += dk
        dq = dq + dot_nn(kt_ref[j], ds)
    d_ref[0, rows_q, :] = (dq.T * SCALE).astype(BF16)
    d_ref[1, rows_q, :] = (dk_ref[rows_q, :] * SCALE).astype(BF16)
    d_ref[2, rows_q, :] = dv_ref[rows_q, :].astype(BF16)


def kernel(
    blocks_ref, count_ref, x_hbm, g_hbm, o_hbm, d_hbm,
    x_ref, g_ref, o_ref, d_ref, kt_ref, vt_ref, s_ref, e_ref, dk_ref, dv_ref, words_ref,
    send_x, send_g, send_o, send_d, recv_x, recv_g, recv_o, recv_d,
):
    pipe, seq, y = lax.axis_index("pipe"), lax.axis_index("seq"), lax.axis_index("head")
    is_owner, section, head = owned_by(pipe, seq, y)
    first_row = pl.multiple_of(seq * BLK + y * ROWS, ROWS)
    mine = pl.ds(first_row, ROWS)

    def send_x_to(i):
        h = (i + seq + 4 * y) % HEADS
        lanes = pl.ds(pl.multiple_of(h * HD, HD), HD)
        return pltpu.make_async_remote_copy(
            src_ref=x_hbm.at[:, :, lanes], dst_ref=x_ref.at[:, mine, :],
            send_sem=send_x, recv_sem=recv_x,
            device_id=owner_of((pipe + 1) % N_PIPE, h), device_id_type=MESH,
        )

    def send_g_to(i):
        h = (i + seq + 4 * y) % HEADS
        lanes = pl.ds(pl.multiple_of(h * HD, HD), HD)
        return pltpu.make_async_remote_copy(
            src_ref=g_hbm.at[:, lanes], dst_ref=g_ref.at[mine, :],
            send_sem=send_g, recv_sem=recv_g,
            device_id=owner_of((pipe + 3) % N_PIPE, h), device_id_type=MESH,
        )

    @pl.loop(0, HEADS)
    def _(i):
        send_x_to(i).start()

    @pl.loop(0, HEADS)
    def _(i):
        send_g_to(i).start()

    def wait_all(ref, sem):
        pltpu.make_async_copy(ref, ref, sem).wait()

    @pl.when(is_owner)
    def _():
        lanes = pl.ds(pl.multiple_of(head * HD, HD), HD)
        kept_words(blocks_ref, count_ref, words_ref)

        def bias(b, j):
            return jnp.where((words_ref[b] & (1 << j)) != 0, 0.0, NEG)

        wait_all(x_ref, recv_x)
        transposed(x_ref, kt_ref, vt_ref)
        for b in range(NT - 1, -1, -1):
            query_tile(
                b, bias, (lambda: wait_all(g_ref, recv_g)) if b == NT - 1 else (lambda: None),
                x_ref, g_ref, kt_ref, vt_ref, s_ref, e_ref, dk_ref, dv_ref, o_ref, d_ref,
            )

            @pl.loop(0, 8)
            def _(i):
                to_seq, to_y = 2 * b + i // 4, i % 4
                rows = pl.ds(pl.multiple_of(to_seq * BLK + to_y * ROWS, ROWS), ROWS)
                pltpu.make_async_remote_copy(
                    src_ref=o_ref.at[rows, :], dst_ref=o_hbm.at[:, lanes],
                    send_sem=send_o, recv_sem=recv_o,
                    device_id=(section, to_seq, to_y), device_id_type=MESH,
                ).start()
                pltpu.make_async_remote_copy(
                    src_ref=d_ref.at[:, rows, :], dst_ref=d_hbm.at[:, :, lanes],
                    send_sem=send_d, recv_sem=recv_d,
                    device_id=(section, to_seq, to_y), device_id_type=MESH,
                ).start()

        wait_all(o_ref, send_o)
        wait_all(d_ref, send_d)

    wait_all(x_hbm, send_x)
    wait_all(g_hbm, send_g)
    wait_all(o_hbm, recv_o)
    wait_all(d_hbm, recv_d)


def body(section_input, grad_input, strided_blocks, strided_count):
    x = jnp.transpose(section_input[0], (1, 0, 2))
    g = grad_input[0]
    hbm = pl.BlockSpec(memory_space=pl.ANY)
    smem = pl.BlockSpec(memory_space=pltpu.SMEM)
    width = HEADS * HD
    out, grads = pl.pallas_call(
        kernel,
        out_shape=(
            jax.ShapeDtypeStruct((ROWS, width), BF16),
            jax.ShapeDtypeStruct((3, ROWS, width), BF16),
        ),
        in_specs=[smem, smem, hbm, hbm],
        out_specs=(hbm, hbm),
        scratch_shapes=[
            pltpu.VMEM((3, SEQ, HD), BF16),
            pltpu.VMEM((SEQ, HD), BF16),
            pltpu.VMEM((SEQ, HD), BF16),
            pltpu.VMEM((3, SEQ, HD), BF16),
            pltpu.VMEM((NT, HD, TILE), BF16),
            pltpu.VMEM((NT, HD, TILE), BF16),
            pltpu.VMEM((NT, TILE, TILE), F32),
            pltpu.VMEM((NT, TILE, TILE), BF16),
            pltpu.VMEM((SEQ, HD), F32),
            pltpu.VMEM((SEQ, HD), F32),
            pltpu.SMEM((NB,), jnp.int32),
        ]
        + [pltpu.SemaphoreType.DMA] * 8,
        compiler_params=pltpu.CompilerParams(has_side_effects=True, vmem_limit_bytes=40 << 20),
    )(strided_blocks, strided_count, x, g)
    return out[None], jnp.transpose(grads, (1, 0, 2))[None]


def solution(mesh):
    in_specs = (P("pipe", ("seq", "head"), None, None), P("pipe", ("seq", "head"), None), P(), P())
    out_specs = (P("pipe", ("seq", "head"), None), P("pipe", ("seq", "head"), None, None))
    return jax.shard_map(body, mesh=mesh, in_specs=in_specs, out_specs=out_specs, check_vma=False)
```

```python
import math

import jax
import jax.numpy as jnp
from jax import lax
from jax.experimental import pallas as pl
from jax.experimental.pallas import tpu as pltpu
from jax.sharding import PartitionSpec as P

HD = 128
BLK = 128
TILE = 256
SEQ = 2048
NB = SEQ // BLK
NT = SEQ // TILE
N_PIPE = 4
N_SEQ = 16
N_HEAD = 4
HEADS = 16
ROWS = 32
SMAX = 14
SCALE = 1.0 / math.sqrt(HD)
SCALE2 = math.log2(math.e) / math.sqrt(HD)
NEG = -1e30
VMEM_LIMIT = 40 * 1024 * 1024
F32 = jnp.float32
BF16 = jnp.bfloat16
MESH = pl.DeviceIdType.MESH


def dot_nt(a, b):
    return lax.dot_general(a, b, (((1,), (1,)), ((), ())), preferred_element_type=F32)


def dot_nn(a, b):
    return lax.dot_general(a, b, (((1,), (0,)), ((), ())), preferred_element_type=F32)


def owner_of(section, head):
    x, y = head // 4, head % 4
    z_lo = 1 - section // 2
    z_hi = (x + (section % 2) * 2 + section // 2) % 4
    return (2 * z_lo + section % 2, x * 4 + z_hi, y)


def owned_by(pipe, seq, y):
    x, z_hi = seq // 4, seq % 4
    half = 1 - pipe // 2
    section = 2 * half + pipe % 2
    is_owner = z_hi == (x + (pipe % 2) * 2 + half) % 4
    return is_owner, section, x * 4 + y


def kept_words(blocks_ref, count_ref, words_ref):
    def one(b, _):
        word = jnp.where(b > 0, jnp.left_shift(1, jnp.maximum(b - 1, 0)), 0)
        for t in range(SMAX):
            bit = jnp.left_shift(1, blocks_ref[b, t])
            word = word | jnp.where(t < count_ref[b], bit, 0)
        words_ref[b] = word
        return 0

    lax.fori_loop(0, NB, one, 0)


def transposed(x_ref, kt_ref, vt_ref):
    def one(j, _):
        rows = pl.ds(pl.multiple_of(j * TILE, TILE), TILE)
        kt_ref[j] = x_ref[1, rows, :].T
        vt_ref[j] = x_ref[2, rows, :].T
        return 0

    lax.fori_loop(0, NT, one, 0)


def query_tile(b, bias, before_grad, x_ref, g_ref, kt_ref, vt_ref, s_ref, e_ref, dk_ref, dv_ref, r_ref):
    rows_q = slice(b * TILE, (b + 1) * TILE)
    q = x_ref[0, rows_q, :]
    lane = lax.broadcasted_iota(jnp.int32, (1, TILE), 1)
    top = jnp.full((8, TILE), NEG, F32)
    for j in range(b + 1):
        s = dot_nt(x_ref[1, j * TILE : (j + 1) * TILE, :], q) * SCALE2
        if j == b:
            key = lax.broadcasted_iota(jnp.int32, (TILE, TILE), 0)
            query = lax.broadcasted_iota(jnp.int32, (TILE, TILE), 1)
            s = jnp.where(key <= query, s, NEG)
        else:
            halves = []
            for half in range(2):
                row = jnp.where(lane < BLK, bias(2 * b, 2 * j + half), bias(2 * b + 1, 2 * j + half))
                halves.append(s[half * BLK : (half + 1) * BLK] + row)
            s = jnp.concatenate(halves, axis=0)
        s_ref[j] = s
        top = jnp.maximum(top, jnp.max(s.reshape(TILE // 8, 8, TILE), axis=0))
    top = jnp.max(top, axis=0, keepdims=True)
    total = jnp.zeros((8, TILE), F32)
    out = jnp.zeros((HD, TILE), F32)
    for j in range(b + 1):
        e = jnp.exp2(s_ref[j] - top)
        total = total + jnp.sum(e.reshape(TILE // 8, 8, TILE), axis=0)
        e = e.astype(BF16)
        e_ref[j] = e
        out = out + dot_nn(vt_ref[j], e)
    inverse = 1.0 / jnp.sum(total, axis=0, keepdims=True)
    out = out * inverse
    before_grad()
    g = g_ref[rows_q, :]
    delta = jnp.sum(out * g.astype(F32).T, axis=0, keepdims=True)
    r_ref[0, rows_q, :] = out.T.astype(BF16)
    dq = jnp.zeros((HD, TILE), F32)
    for j in range(b + 1):
        rows_k = slice(j * TILE, (j + 1) * TILE)
        p = e_ref[j].astype(F32) * inverse
        dp = dot_nt(x_ref[2, rows_k, :], g)
        ds = (p * (dp - delta)).astype(BF16)
        dv = dot_nn(p.astype(BF16), g)
        dk = dot_nn(ds, q)
        if b == NT - 1:
            dv_ref[rows_k, :] = dv
            dk_ref[rows_k, :] = dk
        else:
            dv_ref[rows_k, :] += dv
            dk_ref[rows_k, :] += dk
        dq = dq + dot_nn(kt_ref[j], ds)
    r_ref[1, rows_q, :] = (dq.T * SCALE).astype(BF16)
    r_ref[2, rows_q, :] = (dk_ref[rows_q, :] * SCALE).astype(BF16)
    r_ref[3, rows_q, :] = dv_ref[rows_q, :].astype(BF16)


def kernel(
    blocks_ref, count_ref, x_hbm, g_hbm, r_out,
    x_ref, g_ref, r_ref, kt_ref, vt_ref, s_ref, e_ref, dk_ref, dv_ref, words_ref,
    send_x, send_g, send_r, recv_kv, recv_q, recv_g, recv_r,
):
    pipe, seq, y = lax.axis_index("pipe"), lax.axis_index("seq"), lax.axis_index("head")
    is_owner, section, head = owned_by(pipe, seq, y)
    x, z_hi = seq // 4, seq % 4
    order = (2, 1, 3, 0)
    xs, zs, ys = ([(at + k) % 4 for k in order] for at in (x, z_hi, y))
    after, before = (pipe + 1) % N_PIPE, (pipe + 3) % N_PIPE

    barrier = pltpu.get_barrier_semaphore()

    def ring(device):
        pl.semaphore_signal(barrier, inc=1, device_id=device, device_id_type=MESH)

    def owners(of):
        z_lo, shift = 1 - of // 2, (of % 2) * 2 + of // 2
        for to_x in xs:
            to_seq = to_x * 4 + (to_x + shift) % 4
            for to_y in ys:
                lanes = pl.ds(pl.multiple_of(to_x * (4 * HD) + to_y * HD, HD), HD)
                yield lanes, (2 * z_lo + of % 2, to_seq, to_y)

    @pl.when(is_owner)
    def _():
        for to_z in zs:
            for to_x in xs:
                to_seq = to_x * 4 + to_z
                for to_y in ys:
                    ring(((section + 1) % N_PIPE, to_seq, to_y))
                    ring(((section + 3) % N_PIPE, to_seq, to_y))

    for _, device in owners(pipe):
        ring(device)
    pl.semaphore_wait(barrier, 32 + 64 * is_owner.astype(jnp.int32))

    mine = pl.ds(pl.multiple_of(seq * BLK + y * ROWS, ROWS), ROWS)

    def pass_on(src_ref, dst_ref, send_sem, recv_sem, device):
        pltpu.make_async_remote_copy(
            src_ref=src_ref, dst_ref=dst_ref, send_sem=send_sem, recv_sem=recv_sem,
            device_id=device, device_id_type=MESH,
        ).start()

    for lanes, device in owners(after):
        pass_on(x_hbm.at[1:3, :, lanes], x_ref.at[1:3, mine, :], send_x, recv_kv, device)
    for lanes, device in owners(after):
        pass_on(x_hbm.at[0, :, lanes], x_ref.at[0, mine, :], send_x, recv_q, device)
    for lanes, device in owners(before):
        pass_on(g_hbm.at[:, lanes], g_ref.at[mine, :], send_g, recv_g, device)

    def wait_all(ref, sem):
        pltpu.make_async_copy(ref, ref, sem).wait()

    @pl.when(is_owner)
    def _():
        my_lanes = pl.ds(pl.multiple_of(head * HD, HD), HD)
        kept_words(blocks_ref, count_ref, words_ref)

        def bias(b, j):
            return jnp.where((words_ref[b] & (1 << j)) != 0, 0.0, NEG)

        wait_all(x_ref.at[1:3], recv_kv)
        transposed(x_ref, kt_ref, vt_ref)
        wait_all(x_ref.at[0], recv_q)
        for b in range(NT - 1, -1, -1):
            query_tile(
                b, bias, (lambda: wait_all(g_ref, recv_g)) if b == NT - 1 else (lambda: None),
                x_ref, g_ref, kt_ref, vt_ref, s_ref, e_ref, dk_ref, dv_ref, r_ref,
            )
            for to_y in ys:
                for to_seq in (2 * b, 2 * b + 1):
                    rows = pl.ds(pl.multiple_of(to_seq * BLK + to_y * ROWS, ROWS), ROWS)
                    pass_on(
                        r_ref.at[:, rows, :], r_out.at[:, :, my_lanes], send_r, recv_r,
                        (section, to_seq, to_y),
                    )
        wait_all(r_ref, send_r)

    wait_all(x_hbm, send_x)
    wait_all(g_hbm, send_g)
    wait_all(r_out, recv_r)


def body(section_input, grad_input, strided_blocks, strided_count):
    x = jnp.transpose(section_input[0], (1, 0, 2))
    g = pltpu.with_memory_space_constraint(grad_input[0], pltpu.HBM)
    x = pltpu.with_memory_space_constraint(x, pltpu.HBM)
    hbm = pl.BlockSpec(memory_space=pl.ANY)
    smem = pl.BlockSpec(memory_space=pltpu.SMEM)
    width = HEADS * HD
    result = pl.pallas_call(
        kernel,
        out_shape=jax.ShapeDtypeStruct((4, ROWS, width), BF16),
        in_specs=[smem, smem, hbm, hbm],
        out_specs=hbm,
        scratch_shapes=[
            pltpu.VMEM((3, SEQ, HD), BF16),
            pltpu.VMEM((SEQ, HD), BF16),
            pltpu.VMEM((4, SEQ, HD), BF16),
            pltpu.VMEM((NT, HD, TILE), BF16),
            pltpu.VMEM((NT, HD, TILE), BF16),
            pltpu.VMEM((NT, TILE, TILE), F32),
            pltpu.VMEM((NT, TILE, TILE), BF16),
            pltpu.VMEM((SEQ, HD), F32),
            pltpu.VMEM((SEQ, HD), F32),
            pltpu.SMEM((NB,), jnp.int32),
        ]
        + [pltpu.SemaphoreType.DMA] * 7,
        compiler_params=pltpu.CompilerParams(
            collective_id=0, has_side_effects=True, vmem_limit_bytes=VMEM_LIMIT
        ),
    )(strided_blocks, strided_count, x, g)
    return result[:1], jnp.transpose(result[1:], (1, 0, 2))[None]


def solution(mesh):
    in_specs = (P("pipe", ("seq", "head"), None, None), P("pipe", ("seq", "head"), None), P(), P())
    out_specs = (P("pipe", ("seq", "head"), None), P("pipe", ("seq", "head"), None, None))
    return jax.shard_map(body, mesh=mesh, in_specs=in_specs, out_specs=out_specs, check_vma=False)
```

```python
import math

import jax
import jax.numpy as jnp
from jax import lax
from jax.experimental import pallas as pl
from jax.experimental.pallas import tpu as pltpu
from jax.sharding import PartitionSpec as P

HD = 128
BLK = 128
TILE = 256
SEQ = 2048
NB = SEQ // BLK
NT = SEQ // TILE
N_PIPE = 4
N_SEQ = 16
N_HEAD = 4
HEADS = 16
ROWS = 32
SMAX = 14
SCALE = 1.0 / math.sqrt(HD)
SCALE2 = math.log2(math.e) / math.sqrt(HD)
NEG = -1e30
VMEM_LIMIT = 40 * 1024 * 1024
F32 = jnp.float32
BF16 = jnp.bfloat16
MESH = pl.DeviceIdType.MESH


def dot_nt(a, b):
    return lax.dot_general(a, b, (((1,), (1,)), ((), ())), preferred_element_type=F32)


def dot_nn(a, b):
    return lax.dot_general(a, b, (((1,), (0,)), ((), ())), preferred_element_type=F32)


def owner_of(section, head):
    x, y = head // 4, head % 4
    z_lo = 1 - section // 2
    z_hi = (x + (section % 2) * 2 + section // 2) % 4
    return (2 * z_lo + section % 2, x * 4 + z_hi, y)


def owned_by(pipe, seq, y):
    x, z_hi = seq // 4, seq % 4
    half = 1 - pipe // 2
    section = 2 * half + pipe % 2
    is_owner = z_hi == (x + (pipe % 2) * 2 + half) % 4
    return is_owner, section, x * 4 + y


def kept_words(blocks_ref, count_ref, words_ref):
    def one(b, _):
        word = jnp.where(b > 0, jnp.left_shift(1, jnp.maximum(b - 1, 0)), 0)
        for t in range(SMAX):
            bit = jnp.left_shift(1, blocks_ref[b, t])
            word = word | jnp.where(t < count_ref[b], bit, 0)
        words_ref[b] = word
        return 0

    lax.fori_loop(0, NB, one, 0)


def transposed(x_ref, kt_ref, vt_ref):
    def one(j, _):
        rows = pl.ds(pl.multiple_of(j * TILE, TILE), TILE)
        kt_ref[j] = x_ref[1, rows, :].T
        vt_ref[j] = x_ref[2, rows, :].T
        return 0

    lax.fori_loop(0, NT, one, 0)


def query_tile(b, bias, before_grad, x_ref, g_ref, kt_ref, vt_ref, s_ref, e_ref, dk_ref, dv_ref, r_ref):
    rows_q = slice(b * TILE, (b + 1) * TILE)
    q = x_ref[0, rows_q, :]
    lane = lax.broadcasted_iota(jnp.int32, (1, TILE), 1)
    top = jnp.full((8, TILE), NEG, F32)
    for j in range(b + 1):
        s = dot_nt(x_ref[1, j * TILE : (j + 1) * TILE, :], q) * SCALE2
        if j == b:
            key = lax.broadcasted_iota(jnp.int32, (TILE, TILE), 0)
            query = lax.broadcasted_iota(jnp.int32, (TILE, TILE), 1)
            s = jnp.where(key <= query, s, NEG)
        else:
            halves = []
            for half in range(2):
                row = jnp.where(lane < BLK, bias(2 * b, 2 * j + half), bias(2 * b + 1, 2 * j + half))
                halves.append(s[half * BLK : (half + 1) * BLK] + row)
            s = jnp.concatenate(halves, axis=0)
        s_ref[j] = s
        top = jnp.maximum(top, jnp.max(s.reshape(TILE // 8, 8, TILE), axis=0))
    top = jnp.max(top, axis=0, keepdims=True)
    total = jnp.zeros((8, TILE), F32)
    out = jnp.zeros((HD, TILE), F32)
    for j in range(b + 1):
        e = jnp.exp2(s_ref[j] - top)
        total = total + jnp.sum(e.reshape(TILE // 8, 8, TILE), axis=0)
        e = e.astype(BF16)
        e_ref[j] = e
        out = out + dot_nn(vt_ref[j], e)
    inverse = 1.0 / jnp.sum(total, axis=0, keepdims=True)
    out = out * inverse
    before_grad()
    g = g_ref[rows_q, :]
    delta = jnp.sum(out * g.astype(F32).T, axis=0, keepdims=True)
    r_ref[0, rows_q, :] = out.T.astype(BF16)
    dq = jnp.zeros((HD, TILE), F32)
    for j in range(b + 1):
        rows_k = slice(j * TILE, (j + 1) * TILE)
        p = e_ref[j].astype(F32) * inverse
        dp = dot_nt(x_ref[2, rows_k, :], g)
        ds = (p * (dp - delta)).astype(BF16)
        dv = dot_nn(p.astype(BF16), g)
        dk = dot_nn(ds, q)
        if b == NT - 1:
            dv_ref[rows_k, :] = dv
            dk_ref[rows_k, :] = dk
        else:
            dv_ref[rows_k, :] += dv
            dk_ref[rows_k, :] += dk
        dq = dq + dot_nn(kt_ref[j], ds)
    r_ref[1, rows_q, :] = (dq.T * SCALE).astype(BF16)
    r_ref[2, rows_q, :] = (dk_ref[rows_q, :] * SCALE).astype(BF16)
    r_ref[3, rows_q, :] = dv_ref[rows_q, :].astype(BF16)


def kernel(
    blocks_hbm, count_hbm, x_hbm, g_hbm, r_out,
    x_ref, g_ref, r_ref, kt_ref, vt_ref, s_ref, e_ref, dk_ref, dv_ref, words_ref, blocks_ref, count_ref,
    send_x, send_g, send_r, recv_kv, recv_q, recv_g, recv_r, tables_sem,
):
    pipe, seq, y = lax.axis_index("pipe"), lax.axis_index("seq"), lax.axis_index("head")
    is_owner, section, head = owned_by(pipe, seq, y)
    x, z_hi = seq // 4, seq % 4
    order = (2, 1, 3, 0)
    xs, zs, ys = ([(at + k) % 4 for k in order] for at in (x, z_hi, y))
    after, before = (pipe + 1) % N_PIPE, (pipe + 3) % N_PIPE

    barrier = pltpu.get_barrier_semaphore()

    def ring(device):
        pl.semaphore_signal(barrier, inc=1, device_id=device, device_id_type=MESH)

    def owners(of):
        z_lo, shift = 1 - of // 2, (of % 2) * 2 + of // 2
        for to_x in xs:
            to_seq = to_x * 4 + (to_x + shift) % 4
            for to_y in ys:
                lanes = pl.ds(pl.multiple_of(to_x * (4 * HD) + to_y * HD, HD), HD)
                yield lanes, (2 * z_lo + of % 2, to_seq, to_y)

    for _, device in owners(pipe):
        ring(device)

    @pl.when(is_owner)
    def _():
        for to_z in zs:
            for to_x in xs:
                to_seq = to_x * 4 + to_z
                for to_y in ys:
                    ring(((section + 1) % N_PIPE, to_seq, to_y))
                    ring(((section + 3) % N_PIPE, to_seq, to_y))

    pl.semaphore_wait(barrier, 32 + 64 * is_owner.astype(jnp.int32))

    mine = pl.ds(pl.multiple_of(seq * BLK + y * ROWS, ROWS), ROWS)

    def pass_on(src_ref, dst_ref, send_sem, recv_sem, device):
        pltpu.make_async_remote_copy(
            src_ref=src_ref, dst_ref=dst_ref, send_sem=send_sem, recv_sem=recv_sem,
            device_id=device, device_id_type=MESH,
        ).start()

    for lanes, device in owners(after):
        pass_on(x_hbm.at[1:3, :, lanes], x_ref.at[1:3, mine, :], send_x, recv_kv, device)
    for lanes, device in owners(after):
        pass_on(x_hbm.at[0, :, lanes], x_ref.at[0, mine, :], send_x, recv_q, device)
    for lanes, device in owners(before):
        pass_on(g_hbm.at[:, lanes], g_ref.at[mine, :], send_g, recv_g, device)

    def wait_all(ref, sem):
        pltpu.make_async_copy(ref, ref, sem).wait()

    @pl.when(is_owner)
    def _():
        my_lanes = pl.ds(pl.multiple_of(head * HD, HD), HD)
        for table_hbm, table_ref, k in ((blocks_hbm, blocks_ref, 0), (count_hbm, count_ref, 1)):
            copy = pltpu.make_async_copy(table_hbm, table_ref, tables_sem.at[k])
            copy.start()
            copy.wait()
        kept_words(blocks_ref, count_ref, words_ref)

        def bias(b, j):
            return jnp.where((words_ref[b] & (1 << j)) != 0, 0.0, NEG)

        wait_all(x_ref.at[1:3], recv_kv)
        transposed(x_ref, kt_ref, vt_ref)
        wait_all(x_ref.at[0], recv_q)
        for b in range(NT - 1, -1, -1):
            query_tile(
                b, bias, (lambda: wait_all(g_ref, recv_g)) if b == NT - 1 else (lambda: None),
                x_ref, g_ref, kt_ref, vt_ref, s_ref, e_ref, dk_ref, dv_ref, r_ref,
            )
            for to_y in ys:
                for to_seq in (2 * b, 2 * b + 1):
                    rows = pl.ds(pl.multiple_of(to_seq * BLK + to_y * ROWS, ROWS), ROWS)
                    pass_on(
                        r_ref.at[:, rows, :], r_out.at[:, :, my_lanes], send_r, recv_r,
                        (section, to_seq, to_y),
                    )
        wait_all(r_ref, send_r)

    wait_all(x_hbm, send_x)
    wait_all(g_hbm, send_g)
    wait_all(r_out, recv_r)


def body(section_input, grad_input, strided_blocks, strided_count):
    operands = (strided_blocks, strided_count, jnp.transpose(section_input[0], (1, 0, 2)), grad_input[0])
    operands = [pltpu.with_memory_space_constraint(operand, pltpu.HBM) for operand in operands]
    hbm = pl.BlockSpec(memory_space=pl.ANY)
    width = HEADS * HD
    result = pl.pallas_call(
        kernel,
        out_shape=jax.ShapeDtypeStruct((4, ROWS, width), BF16),
        in_specs=[hbm] * 4,
        out_specs=hbm,
        scratch_shapes=[
            pltpu.VMEM((3, SEQ, HD), BF16),
            pltpu.VMEM((SEQ, HD), BF16),
            pltpu.VMEM((4, SEQ, HD), BF16),
            pltpu.VMEM((NT, HD, TILE), BF16),
            pltpu.VMEM((NT, HD, TILE), BF16),
            pltpu.VMEM((NT, TILE, TILE), F32),
            pltpu.VMEM((NT, TILE, TILE), BF16),
            pltpu.VMEM((SEQ, HD), F32),
            pltpu.VMEM((SEQ, HD), F32),
            pltpu.SMEM((NB,), jnp.int32),
            pltpu.SMEM((NB, SMAX), jnp.int32),
            pltpu.SMEM((NB,), jnp.int32),
        ]
        + [pltpu.SemaphoreType.DMA] * 7
        + [pltpu.SemaphoreType.DMA((2,))],
        compiler_params=pltpu.CompilerParams(
            collective_id=0, has_side_effects=True, vmem_limit_bytes=VMEM_LIMIT
        ),
    )(*operands)
    return result[:1], jnp.transpose(result[1:], (1, 0, 2))[None]


def solution(mesh):
    in_specs = (P("pipe", ("seq", "head"), None, None), P("pipe", ("seq", "head"), None), P(), P())
    out_specs = (P("pipe", ("seq", "head"), None), P("pipe", ("seq", "head"), None, None))
    return jax.shard_map(body, mesh=mesh, in_specs=in_specs, out_specs=out_specs, check_vma=False)
```

```python
import math

import jax
import jax.numpy as jnp
from jax import lax
from jax.experimental import pallas as pl
from jax.experimental.pallas import tpu as pltpu
from jax.sharding import PartitionSpec as P

HD = 128
BLK = 128
TILE = 256
SEQ = 2048
NB = SEQ // BLK
NT = SEQ // TILE
N_PIPE = 4
N_SEQ = 16
N_HEAD = 4
HEADS = 16
ROWS = 32
SMAX = 14
SCALE = 1.0 / math.sqrt(HD)
SCALE2 = math.log2(math.e) / math.sqrt(HD)
NEG = -1e30
VMEM_LIMIT = 40 * 1024 * 1024
F32 = jnp.float32
BF16 = jnp.bfloat16
MESH = pl.DeviceIdType.MESH


def dot_nt(a, b):
    return lax.dot_general(a, b, (((1,), (1,)), ((), ())), preferred_element_type=F32)


def dot_nn(a, b):
    return lax.dot_general(a, b, (((1,), (0,)), ((), ())), preferred_element_type=F32)


def owner_of(section, head):
    x, y = head // 4, head % 4
    z_lo = 1 - section // 2
    z_hi = (x + (section % 2) * 2 + section // 2) % 4
    return (2 * z_lo + section % 2, x * 4 + z_hi, y)


def owned_by(pipe, seq, y):
    x, z_hi = seq // 4, seq % 4
    half = 1 - pipe // 2
    section = 2 * half + pipe % 2
    is_owner = z_hi == (x + (pipe % 2) * 2 + half) % 4
    return is_owner, section, x * 4 + y


def kept_words(blocks_ref, count_ref, words_ref):
    def one(b, _):
        word = jnp.where(b > 0, jnp.left_shift(1, jnp.maximum(b - 1, 0)), 0)
        for t in range(SMAX):
            bit = jnp.left_shift(1, blocks_ref[b, t])
            word = word | jnp.where(t < count_ref[b], bit, 0)
        words_ref[b] = word
        return 0

    lax.fori_loop(0, NB, one, 0)


def transposed(x_ref, kt_ref, vt_ref):
    def one(j, _):
        rows = pl.ds(pl.multiple_of(j * TILE, TILE), TILE)
        kt_ref[j] = x_ref[1, rows, :].T
        vt_ref[j] = x_ref[2, rows, :].T
        return 0

    lax.fori_loop(0, NT, one, 0)


def query_tile(b, bias, before_grad, x_ref, g_ref, kt_ref, vt_ref, s_ref, e_ref, dk_ref, dv_ref, r_ref):
    rows_q = slice(b * TILE, (b + 1) * TILE)
    q = x_ref[0, rows_q, :]
    lane = lax.broadcasted_iota(jnp.int32, (1, TILE), 1)
    top = jnp.full((8, TILE), NEG, F32)
    for j in range(b + 1):
        s = dot_nt(x_ref[1, j * TILE : (j + 1) * TILE, :], q) * SCALE2
        if j == b:
            key = lax.broadcasted_iota(jnp.int32, (TILE, TILE), 0)
            query = lax.broadcasted_iota(jnp.int32, (TILE, TILE), 1)
            s = jnp.where(key <= query, s, NEG)
        else:
            halves = []
            for half in range(2):
                row = jnp.where(lane < BLK, bias(2 * b, 2 * j + half), bias(2 * b + 1, 2 * j + half))
                halves.append(s[half * BLK : (half + 1) * BLK] + row)
            s = jnp.concatenate(halves, axis=0)
        s_ref[j] = s
        top = jnp.maximum(top, jnp.max(s.reshape(TILE // 8, 8, TILE), axis=0))
    top = jnp.max(top, axis=0, keepdims=True)
    total = jnp.zeros((8, TILE), F32)
    out = jnp.zeros((HD, TILE), F32)
    for j in range(b + 1):
        e = jnp.exp2(s_ref[j] - top)
        total = total + jnp.sum(e.reshape(TILE // 8, 8, TILE), axis=0)
        e = e.astype(BF16)
        e_ref[j] = e
        out = out + dot_nn(vt_ref[j], e)
    inverse = 1.0 / jnp.sum(total, axis=0, keepdims=True)
    out = out * inverse
    before_grad()
    g = g_ref[rows_q, :]
    delta = jnp.sum(out * g.astype(F32).T, axis=0, keepdims=True)
    r_ref[0, rows_q, :] = out.T.astype(BF16)
    dq = jnp.zeros((HD, TILE), F32)
    for j in range(b + 1):
        rows_k = slice(j * TILE, (j + 1) * TILE)
        p = e_ref[j].astype(F32) * inverse
        dp = dot_nt(x_ref[2, rows_k, :], g)
        ds = (p * (dp - delta)).astype(BF16)
        dv = dot_nn(p.astype(BF16), g)
        dk = dot_nn(ds, q)
        if b == NT - 1:
            dv_ref[rows_k, :] = dv
            dk_ref[rows_k, :] = dk
        else:
            dv_ref[rows_k, :] += dv
            dk_ref[rows_k, :] += dk
        dq = dq + dot_nn(kt_ref[j], ds)
    r_ref[1, rows_q, :] = (dq.T * SCALE).astype(BF16)
    r_ref[2, rows_q, :] = (dk_ref[rows_q, :] * SCALE).astype(BF16)
    r_ref[3, rows_q, :] = dv_ref[rows_q, :].astype(BF16)


def kernel(
    blocks_hbm, count_hbm, x_hbm, g_hbm, r_out,
    x_ref, g_ref, r_ref, kt_ref, vt_ref, s_ref, e_ref, dk_ref, dv_ref, words_ref, blocks_ref, count_ref,
    send_x, send_g, send_r, recv_kv, recv_q, recv_g, recv_r, tables_sem,
):
    pipe, seq, y = lax.axis_index("pipe"), lax.axis_index("seq"), lax.axis_index("head")
    is_owner, section, head = owned_by(pipe, seq, y)
    x, z_hi = seq // 4, seq % 4
    order = (2, 1, 3, 0)
    xs, zs, ys = ([(at + k) % 4 for k in order] for at in (x, z_hi, y))
    after, before = (pipe + 1) % N_PIPE, (pipe + 3) % N_PIPE

    barrier = pltpu.get_barrier_semaphore()

    def ring(device):
        pl.semaphore_signal(barrier, inc=1, device_id=device, device_id_type=MESH)

    def owners(of):
        z_lo, shift = 1 - of // 2, (of % 2) * 2 + of // 2
        for to_y in ys:
            for to_x in xs:
                to_seq = to_x * 4 + (to_x + shift) % 4
                lanes = pl.ds(pl.multiple_of(to_x * (4 * HD) + to_y * HD, HD), HD)
                yield lanes, (2 * z_lo + of % 2, to_seq, to_y)

    for _, device in owners(pipe):
        ring(device)

    @pl.when(is_owner)
    def _():
        for to_z in zs:
            for to_x in xs:
                to_seq = to_x * 4 + to_z
                for to_y in ys:
                    ring(((section + 1) % N_PIPE, to_seq, to_y))
                    ring(((section + 3) % N_PIPE, to_seq, to_y))

    pl.semaphore_wait(barrier, 32 + 64 * is_owner.astype(jnp.int32))

    mine = pl.ds(pl.multiple_of(seq * BLK + y * ROWS, ROWS), ROWS)

    def pass_on(src_ref, dst_ref, send_sem, recv_sem, device):
        pltpu.make_async_remote_copy(
            src_ref=src_ref, dst_ref=dst_ref, send_sem=send_sem, recv_sem=recv_sem,
            device_id=device, device_id_type=MESH,
        ).start()

    for lanes, device in owners(after):
        pass_on(x_hbm.at[1:3, :, lanes], x_ref.at[1:3, mine, :], send_x, recv_kv, device)
    for lanes, device in owners(after):
        pass_on(x_hbm.at[0, :, lanes], x_ref.at[0, mine, :], send_x, recv_q, device)
    for lanes, device in owners(before):
        pass_on(g_hbm.at[:, lanes], g_ref.at[mine, :], send_g, recv_g, device)

    def wait_all(ref, sem):
        pltpu.make_async_copy(ref, ref, sem).wait()

    @pl.when(is_owner)
    def _():
        my_lanes = pl.ds(pl.multiple_of(head * HD, HD), HD)
        for table_hbm, table_ref, k in ((blocks_hbm, blocks_ref, 0), (count_hbm, count_ref, 1)):
            copy = pltpu.make_async_copy(table_hbm, table_ref, tables_sem.at[k])
            copy.start()
            copy.wait()
        kept_words(blocks_ref, count_ref, words_ref)

        def bias(b, j):
            return jnp.where((words_ref[b] & (1 << j)) != 0, 0.0, NEG)

        wait_all(x_ref.at[1:3], recv_kv)
        transposed(x_ref, kt_ref, vt_ref)
        wait_all(x_ref.at[0], recv_q)
        for b in range(NT - 1, -1, -1):
            query_tile(
                b, bias, (lambda: wait_all(g_ref, recv_g)) if b == NT - 1 else (lambda: None),
                x_ref, g_ref, kt_ref, vt_ref, s_ref, e_ref, dk_ref, dv_ref, r_ref,
            )
            for to_y in ys:
                for to_seq in (2 * b, 2 * b + 1):
                    rows = pl.ds(pl.multiple_of(to_seq * BLK + to_y * ROWS, ROWS), ROWS)
                    pass_on(
                        r_ref.at[:, rows, :], r_out.at[:, :, my_lanes], send_r, recv_r,
                        (section, to_seq, to_y),
                    )
        wait_all(r_ref, send_r)

    wait_all(x_hbm, send_x)
    wait_all(g_hbm, send_g)
    wait_all(r_out, recv_r)


def body(section_input, grad_input, strided_blocks, strided_count):
    operands = (strided_blocks, strided_count, jnp.transpose(section_input[0], (1, 0, 2)), grad_input[0])
    operands = [pltpu.with_memory_space_constraint(operand, pltpu.HBM) for operand in operands]
    hbm = pl.BlockSpec(memory_space=pl.ANY)
    width = HEADS * HD
    result = pl.pallas_call(
        kernel,
        out_shape=jax.ShapeDtypeStruct((4, ROWS, width), BF16),
        in_specs=[hbm] * 4,
        out_specs=hbm,
        scratch_shapes=[
            pltpu.VMEM((3, SEQ, HD), BF16),
            pltpu.VMEM((SEQ, HD), BF16),
            pltpu.VMEM((4, SEQ, HD), BF16),
            pltpu.VMEM((NT, HD, TILE), BF16),
            pltpu.VMEM((NT, HD, TILE), BF16),
            pltpu.VMEM((NT, TILE, TILE), F32),
            pltpu.VMEM((NT, TILE, TILE), BF16),
            pltpu.VMEM((SEQ, HD), F32),
            pltpu.VMEM((SEQ, HD), F32),
            pltpu.SMEM((NB,), jnp.int32),
            pltpu.SMEM((NB, SMAX), jnp.int32),
            pltpu.SMEM((NB,), jnp.int32),
        ]
        + [pltpu.SemaphoreType.DMA] * 7
        + [pltpu.SemaphoreType.DMA((2,))],
        compiler_params=pltpu.CompilerParams(
            collective_id=0, has_side_effects=True, vmem_limit_bytes=VMEM_LIMIT
        ),
    )(*operands)
    return result[:1], jnp.transpose(result[1:], (1, 0, 2))[None]


def solution(mesh):
    in_specs = (P("pipe", ("seq", "head"), None, None), P("pipe", ("seq", "head"), None), P(), P())
    out_specs = (P("pipe", ("seq", "head"), None), P("pipe", ("seq", "head"), None, None))
    return jax.shard_map(body, mesh=mesh, in_specs=in_specs, out_specs=out_specs, check_vma=False)
```

```python
import math

import jax
import jax.numpy as jnp
from jax import lax
from jax.experimental import pallas as pl
from jax.experimental.pallas import tpu as pltpu
from jax.sharding import PartitionSpec as P

HD = 128
BLK = 128
TILE = 256
SEQ = 2048
NB = SEQ // BLK
NT = SEQ // TILE
N_PIPE = 4
N_SEQ = 16
N_HEAD = 4
HEADS = 16
ROWS = 32
SMAX = 14
SCALE = 1.0 / math.sqrt(HD)
SCALE2 = math.log2(math.e) / math.sqrt(HD)
NEG = -1e30
VMEM_LIMIT = 40 * 1024 * 1024
F32 = jnp.float32
BF16 = jnp.bfloat16
MESH = pl.DeviceIdType.MESH


def dot_nt(a, b):
    return lax.dot_general(a, b, (((1,), (1,)), ((), ())), preferred_element_type=F32)


def dot_nn(a, b):
    return lax.dot_general(a, b, (((1,), (0,)), ((), ())), preferred_element_type=F32)


def place_of(section):
    return section + 0


def owner_of(section, x, y):
    z_lo, z_hi = (x + y) % 2, (x + place_of(section)) % 4
    return (2 * z_lo + section % 2, x * 4 + z_hi, y)


def owned_by(pipe, seq, y):
    x, z_hi = seq // 4, seq % 4
    section = place_of((z_hi + 4 - x) % 4)
    is_owner = (section % 2 == pipe % 2) & ((x + y) % 2 == pipe // 2)
    return is_owner, section, x * 4 + y


def kept_words(blocks_ref, count_ref, words_ref):
    def one(b, _):
        word = jnp.where(b > 0, jnp.left_shift(1, jnp.maximum(b - 1, 0)), 0)
        for t in range(SMAX):
            bit = jnp.left_shift(1, blocks_ref[b, t])
            word = word | jnp.where(t < count_ref[b], bit, 0)
        words_ref[b] = word
        return 0

    lax.fori_loop(0, NB, one, 0)


def transposed(x_ref, kt_ref, vt_ref):
    def one(j, _):
        rows = pl.ds(pl.multiple_of(j * TILE, TILE), TILE)
        kt_ref[j] = x_ref[1, rows, :].T
        vt_ref[j] = x_ref[2, rows, :].T
        return 0

    lax.fori_loop(0, NT, one, 0)


def query_tile(b, bias, before_grad, x_ref, g_ref, kt_ref, vt_ref, s_ref, e_ref, dk_ref, dv_ref, r_ref):
    rows_q = slice(b * TILE, (b + 1) * TILE)
    q = x_ref[0, rows_q, :]
    lane = lax.broadcasted_iota(jnp.int32, (1, TILE), 1)
    top = jnp.full((8, TILE), NEG, F32)
    for j in range(b + 1):
        s = dot_nt(x_ref[1, j * TILE : (j + 1) * TILE, :], q) * SCALE2
        if j == b:
            key = lax.broadcasted_iota(jnp.int32, (TILE, TILE), 0)
            query = lax.broadcasted_iota(jnp.int32, (TILE, TILE), 1)
            s = jnp.where(key <= query, s, NEG)
        else:
            halves = []
            for half in range(2):
                row = jnp.where(lane < BLK, bias(2 * b, 2 * j + half), bias(2 * b + 1, 2 * j + half))
                halves.append(s[half * BLK : (half + 1) * BLK] + row)
            s = jnp.concatenate(halves, axis=0)
        s_ref[j] = s
        top = jnp.maximum(top, jnp.max(s.reshape(TILE // 8, 8, TILE), axis=0))
    top = jnp.max(top, axis=0, keepdims=True)
    total = jnp.zeros((8, TILE), F32)
    out = jnp.zeros((HD, TILE), F32)
    for j in range(b + 1):
        e = jnp.exp2(s_ref[j] - top)
        total = total + jnp.sum(e.reshape(TILE // 8, 8, TILE), axis=0)
        e = e.astype(BF16)
        e_ref[j] = e
        out = out + dot_nn(vt_ref[j], e)
    inverse = 1.0 / jnp.sum(total, axis=0, keepdims=True)
    out = out * inverse
    before_grad()
    g = g_ref[rows_q, :]
    delta = jnp.sum(out * g.astype(F32).T, axis=0, keepdims=True)
    r_ref[0, rows_q, :] = out.T.astype(BF16)
    dq = jnp.zeros((HD, TILE), F32)
    for j in range(b + 1):
        rows_k = slice(j * TILE, (j + 1) * TILE)
        p = e_ref[j].astype(F32) * inverse
        dp = dot_nt(x_ref[2, rows_k, :], g)
        ds = (p * (dp - delta)).astype(BF16)
        dv = dot_nn(p.astype(BF16), g)
        dk = dot_nn(ds, q)
        if b == NT - 1:
            dv_ref[rows_k, :] = dv
            dk_ref[rows_k, :] = dk
        else:
            dv_ref[rows_k, :] += dv
            dk_ref[rows_k, :] += dk
        dq = dq + dot_nn(kt_ref[j], ds)
    r_ref[1, rows_q, :] = (dq.T * SCALE).astype(BF16)
    r_ref[2, rows_q, :] = (dk_ref[rows_q, :] * SCALE).astype(BF16)
    r_ref[3, rows_q, :] = dv_ref[rows_q, :].astype(BF16)


def kernel(
    blocks_hbm, count_hbm, x_hbm, g_hbm, r_out,
    x_ref, g_ref, r_ref, kt_ref, vt_ref, s_ref, e_ref, dk_ref, dv_ref, words_ref, blocks_ref, count_ref,
    send_x, send_g, send_r, recv_kv, recv_q, recv_g, recv_r, tables_sem,
):
    pipe, seq, y = lax.axis_index("pipe"), lax.axis_index("seq"), lax.axis_index("head")
    is_owner, section, head = owned_by(pipe, seq, y)
    x, z_hi = seq // 4, seq % 4
    order = (2, 1, 3, 0)
    xs, zs, ys = ([(at + k) % 4 for k in order] for at in (x, z_hi, y))
    after, before = (pipe + 1) % N_PIPE, (pipe + 3) % N_PIPE

    barrier = pltpu.get_barrier_semaphore()

    def ring(device):
        pl.semaphore_signal(barrier, inc=1, device_id=device, device_id_type=MESH)

    def owners(of):
        for to_x in xs:
            for to_y in ys:
                lanes = pl.ds(pl.multiple_of(to_x * (4 * HD) + to_y * HD, HD), HD)
                yield lanes, owner_of(of, to_x, to_y)

    owner = is_owner.astype(jnp.int32)
    own = owner * (section == pipe).astype(jnp.int32)
    *others, (_, last) = owners(pipe)
    for _, device in others:
        ring(device)

    @pl.when(own == 0)
    def _():
        ring(last)

    @pl.when(is_owner)
    def _():
        for to_z in zs:
            for to_x in xs:
                to_seq = to_x * 4 + to_z
                for to_y in ys:
                    ring(((section + 1) % N_PIPE, to_seq, to_y))
                    ring(((section + 3) % N_PIPE, to_seq, to_y))

    pl.semaphore_wait(barrier, 32 + 64 * owner - own)

    mine = pl.ds(pl.multiple_of(seq * BLK + y * ROWS, ROWS), ROWS)

    def pass_on(src_ref, dst_ref, send_sem, recv_sem, device):
        pltpu.make_async_remote_copy(
            src_ref=src_ref, dst_ref=dst_ref, send_sem=send_sem, recv_sem=recv_sem,
            device_id=device, device_id_type=MESH,
        ).start()

    for lanes, device in owners(after):
        pass_on(x_hbm.at[1:3, :, lanes], x_ref.at[1:3, mine, :], send_x, recv_kv, device)
    for lanes, device in owners(after):
        pass_on(x_hbm.at[0, :, lanes], x_ref.at[0, mine, :], send_x, recv_q, device)
    for lanes, device in owners(before):
        pass_on(g_hbm.at[:, lanes], g_ref.at[mine, :], send_g, recv_g, device)

    def wait_all(ref, sem):
        pltpu.make_async_copy(ref, ref, sem).wait()

    @pl.when(is_owner)
    def _():
        my_lanes = pl.ds(pl.multiple_of(head * HD, HD), HD)
        for table_hbm, table_ref, k in ((blocks_hbm, blocks_ref, 0), (count_hbm, count_ref, 1)):
            copy = pltpu.make_async_copy(table_hbm, table_ref, tables_sem.at[k])
            copy.start()
            copy.wait()
        kept_words(blocks_ref, count_ref, words_ref)

        def bias(b, j):
            return jnp.where((words_ref[b] & (1 << j)) != 0, 0.0, NEG)

        wait_all(x_ref.at[1:3], recv_kv)
        transposed(x_ref, kt_ref, vt_ref)
        wait_all(x_ref.at[0], recv_q)
        for b in range(NT - 1, -1, -1):
            query_tile(
                b, bias, (lambda: wait_all(g_ref, recv_g)) if b == NT - 1 else (lambda: None),
                x_ref, g_ref, kt_ref, vt_ref, s_ref, e_ref, dk_ref, dv_ref, r_ref,
            )
            for to_y in ys:
                for to_seq in (2 * b, 2 * b + 1):
                    rows = pl.ds(pl.multiple_of(to_seq * BLK + to_y * ROWS, ROWS), ROWS)
                    piece, place = r_ref.at[:, rows, :], r_out.at[:, :, my_lanes]
                    if to_y is not ys[-1]:
                        pass_on(piece, place, send_r, recv_r, (section, to_seq, to_y))
                        continue
                    here = own * (seq == to_seq).astype(jnp.int32)

                    @pl.when(here == 0)
                    def _():
                        pass_on(piece, place, send_r, recv_r, (section, to_seq, to_y))

                    @pl.when(here == 1)
                    def _():
                        pltpu.make_async_copy(piece, place, recv_r).start()

        @pl.when(own == 0)
        def _():
            wait_all(r_ref, send_r)

        @pl.when(own == 1)
        def _():
            wait_all(r_ref.at[:, pl.ds(ROWS, SEQ - ROWS), :], send_r)

    wait_all(x_hbm, send_x)
    wait_all(g_hbm, send_g)
    wait_all(r_out, recv_r)


def body(section_input, grad_input, strided_blocks, strided_count):
    operands = (strided_blocks, strided_count, jnp.transpose(section_input[0], (1, 0, 2)), grad_input[0])
    operands = [pltpu.with_memory_space_constraint(operand, pltpu.HBM) for operand in operands]
    hbm = pl.BlockSpec(memory_space=pl.ANY)
    width = HEADS * HD
    result = pl.pallas_call(
        kernel,
        out_shape=jax.ShapeDtypeStruct((4, ROWS, width), BF16),
        in_specs=[hbm] * 4,
        out_specs=hbm,
        scratch_shapes=[
            pltpu.VMEM((3, SEQ, HD), BF16),
            pltpu.VMEM((SEQ, HD), BF16),
            pltpu.VMEM((4, SEQ, HD), BF16),
            pltpu.VMEM((NT, HD, TILE), BF16),
            pltpu.VMEM((NT, HD, TILE), BF16),
            pltpu.VMEM((NT, TILE, TILE), F32),
            pltpu.VMEM((NT, TILE, TILE), BF16),
            pltpu.VMEM((SEQ, HD), F32),
            pltpu.VMEM((SEQ, HD), F32),
            pltpu.SMEM((NB,), jnp.int32),
            pltpu.SMEM((NB, SMAX), jnp.int32),
            pltpu.SMEM((NB,), jnp.int32),
        ]
        + [pltpu.SemaphoreType.DMA] * 7
        + [pltpu.SemaphoreType.DMA((2,))],
        compiler_params=pltpu.CompilerParams(
            collective_id=0, has_side_effects=True, vmem_limit_bytes=VMEM_LIMIT
        ),
    )(*operands)
    return result[:1], jnp.transpose(result[1:], (1, 0, 2))[None]


def solution(mesh):
    in_specs = (P("pipe", ("seq", "head"), None, None), P("pipe", ("seq", "head"), None), P(), P())
    out_specs = (P("pipe", ("seq", "head"), None), P("pipe", ("seq", "head"), None, None))
    return jax.shard_map(body, mesh=mesh, in_specs=in_specs, out_specs=out_specs, check_vma=False)
```
